32 devices in a mesh: nodes: 32 (over z, y, x, core).
Axes of the slice: x: 2, y: 2, z: 4, core: 2. Of those that a mesh axis runs over, the one named last changes fastest.
Arguments:
- rhs: bfloat16 [4, 20480, 256], P(None, 'nodes'), may hold values from -6 to 6
- inv_diag: bfloat16 [4, 20480, 640], P(None, 'nodes'), as said below
- factor: bfloat16 [3, 49152, 640], P(None, 'nodes'), may hold values from -0.15625 to 0.15625
- tile_list: int32 [3, 32, 12], P(None, 'nodes'), may hold values from 0 to 239, as said below
- live_count: int32 [3, 32], P(None, 'nodes'), may hold values from 4 to 12, as said below
Outputs:
- solution: float32 [4, 20480, 256], P(None, 'nodes')
The draws below stay inside these ranges and needn't reach their ends.
Inputs may be any that keep to these rules, and one draw needn't show every extreme that they name: `tile_list`: entries at first index i name tiles of levels 0 to i only: they are below (i + 1) * 2 * 8 * 5. `live_count`: in every level some supernode has all 12 slots in use. `inv_diag`: each 640 by 640 block is upper triangular: zero below its diagonal, diagonal entries between 0.5 and 2.
All inputs are finite; a program needn't handle non-finite values.
Results may differ from the reference program's by a relative error of at most 0.004.
Values may be sent and summed in bfloat16 or wider, within the bound.
No kernel may reach another device: no remote copies, remote signals or barrier semaphores. Data moves between devices by JAX's collectives and lax.ppermute only.
A program may use at most 128 MiB of HBM per device.

```python
import math
import jax
import jax.numpy as jnp
from jax import lax

W = 640
K = 256
TILE = 128
LEVELS = 4
SLOTS = 12
GROUP = 8
SUPERNODES = 32


def draw_inv_diag(key, part):
    key_upper, key_diag = jax.random.split(jax.random.fold_in(key, 11), 2)
    shape = (LEVELS, SUPERNODES, W, W)
    upper = jax.random.normal(key_upper, shape, jnp.float32)
    upper = jnp.triu(upper, 1) * (0.8 / math.sqrt(W))
    logs = jax.random.uniform(key_diag, (LEVELS, SUPERNODES, W), jnp.float32, math.log(0.5), math.log(2.0))
    blocks = upper + jnp.exp(logs)[..., None] * jnp.eye(W, dtype=jnp.float32)
    return blocks.reshape(LEVELS, SUPERNODES * W, W).astype(jnp.bfloat16)


def draw_tile_list(key, part):
    raw_values = jax.random.randint(jax.random.fold_in(key, 23), (LEVELS - 1, SUPERNODES, SLOTS), 0, 1048576)
    limits = (jnp.arange(LEVELS - 1, dtype=jnp.int32) + 1) * (2 * GROUP * (W // TILE))
    return (raw_values % limits[:, None, None]).astype(jnp.int32)


def draw_live_count(key, part):
    key_small, key_full, key_place = jax.random.split(jax.random.fold_in(key, 37), 3)
    small_counts = jax.random.randint(key_small, (LEVELS - 1, SUPERNODES), SLOTS // 3, 3 * SLOTS // 4 + 1)
    full_rows = jax.random.randint(key_full, (LEVELS - 1, SUPERNODES), 0, 8) == 0
    places = jax.random.randint(key_place, (LEVELS - 1,), 0, SUPERNODES)
    forced = jnp.arange(SUPERNODES, dtype=jnp.int32)[None, :] == places[:, None]
    counts = jnp.where(full_rows | forced, SLOTS, small_counts)
    return counts.astype(jnp.int32)


def steps_of(key, shape, cuts, least, largest):
    factor_of = 1.0
    for position, parts in cuts:
        draws = jax.random.uniform(jax.random.fold_in(jax.random.fold_in(key, 6), position), (parts,), jnp.float32, least / len(cuts), largest / len(cuts))
        factor_of = factor_of * jnp.repeat(jnp.exp(draws), shape[position] // parts).reshape((-1,) + (1,) * (len(shape) - 1 - position))
    return factor_of


def normal_values(rng, shape, deviation, reach, cuts=(), kind=jnp.bfloat16):
    drawn = deviation * jax.random.normal(rng, shape, jnp.float32)
    if cuts:
        drawn = drawn * steps_of(rng, shape, cuts, -0.22, 0.18)
    return jnp.clip(drawn, -reach, reach).astype(kind)


def setup_inputs(seed: int = 0) -> dict:
    arg_keys = jax.random.split(jax.random.key(seed), 6)
    return {
        "rhs": normal_values(arg_keys[0], (LEVELS, SUPERNODES * W, K), 1.0, 6.0, ((1, 32),)),
        "inv_diag": draw_inv_diag(jax.random.fold_in(arg_keys[5], 71), 0),
        "factor": normal_values(arg_keys[2], (LEVELS - 1, SUPERNODES * SLOTS * TILE, W), (SLOTS * TILE) ** -0.5, 0.15625, ((1, 32),)),
        "tile_list": draw_tile_list(jax.random.fold_in(arg_keys[5], 71), 0),
        "live_count": draw_live_count(jax.random.fold_in(arg_keys[5], 71), 0),
    }


def reference(rhs, inv_diag, factor, tile_list, live_count):
    per_node = W // TILE
    groups = SUPERNODES // GROUP
    pooled = []
    solved_all = []
    for height in range(LEVELS):
        updated = rhs[height].astype(jnp.float32)
        if height > 0:
            pool = jnp.concatenate(pooled, axis=1)
            factor_tiles = factor[height - 1].reshape(groups, GROUP, SLOTS, TILE, W)
            indices = tile_list[height - 1].reshape(groups, GROUP, SLOTS)
            counts = live_count[height - 1].reshape(groups, GROUP)

            def one_group(operands):
                pool_group, factor_group, index_group, count_group = operands
                picked = pool_group[index_group].astype(jnp.float32)
                live_mask = (jnp.arange(SLOTS)[None, :] < count_group[:, None]).astype(jnp.float32)
                picked = picked * live_mask[:, :, None, None]
                return jnp.einsum("gstw,gstk->gwk", factor_group.astype(jnp.float32), picked)

            change = lax.map(one_group, (pool, factor_tiles, indices, counts))
            updated = updated - change.reshape(SUPERNODES * W, K)
        rounded = updated.astype(jnp.bfloat16)
        blocks = inv_diag[height].reshape(SUPERNODES, W, W).astype(jnp.float32)
        solution = jnp.einsum("swv,svk->swk", blocks, rounded.reshape(SUPERNODES, W, K).astype(jnp.float32))
        solution = solution.reshape(SUPERNODES * W, K)
        solved_all.append(solution)
        if height < LEVELS - 1:
            own_group = solution.astype(jnp.bfloat16).reshape(groups, GROUP * per_node, TILE, K)
            pooled.append(jnp.concatenate([jnp.roll(own_group, 1, axis=0), own_group], axis=1))
    return jnp.stack(solved_all)
```

```python
import functools

import jax
import jax.numpy as jnp
from jax import lax
from jax.experimental import pallas as pl
from jax.experimental.pallas import tpu as pltpu
from jax.sharding import PartitionSpec as P

GROUP = 8
CORES = 2
CHIPS = GROUP // CORES
STREAMS = 1


VMEM = pl.BlockSpec(memory_space=pltpu.VMEM)
SMEM = pl.BlockSpec(memory_space=pltpu.SMEM)


def send(value, hop, step=0):
    size = lax.axis_size("nodes")
    route = [(i, ((i ^ (hop * CORES)) + step * GROUP) % size) for i in range(size)]
    return lax.ppermute(value, "nodes", route)


def swap(value):
    size = lax.axis_size("nodes")
    return lax.ppermute(value, "nodes", [(i, i ^ 1) for i in range(size)])


def solve_rows(inv_ref, reduced_ref, x_ref, piece_refs, chip, tile):
    width = inv_ref.shape[0]
    per_node = width // tile
    quarter = tile // CHIPS
    for i in range(per_node):
        rows = pl.ds(i * tile, tile)
        x = jnp.dot(
            inv_ref[i * tile : (i + 1) * tile, i * tile :],
            reduced_ref[i * tile :, :],
            preferred_element_type=jnp.float32,
        )
        x_ref[rows, :] = x
    for relative, piece_ref in enumerate(piece_refs):
        first = (chip ^ relative) * quarter
        for i in range(per_node):
            start = pl.multiple_of(i * tile + first, quarter)
            piece_ref[i] = x_ref[pl.ds(start, quarter), :].astype(jnp.bfloat16)


def first_kernel(tile, info_ref, rhs_ref, inv_ref, x_ref, *piece_refs):
    solve_rows(inv_ref, rhs_ref, x_ref, piece_refs, info_ref[0], tile)


def level_kernel(tile, info_ref, rhs_ref, factor_ref, inv_ref, *refs):
    parts, refs = refs[:CHIPS], refs[CHIPS:]
    x_ref, piece_refs = refs[0], refs[1:-2]
    picked_ref, reduced_ref = refs[-2:]
    chip, count = info_ref[0], info_ref[1]
    slots, quarter = parts[0].shape[:2]
    for relative, part in enumerate(parts):
        first = (chip ^ relative) * quarter
        for slot in range(slots):
            start = pl.multiple_of(slot * tile + first, quarter)
            value = part[slot]
            picked_ref[pl.ds(start, quarter), :] = jnp.where(
                slot < count, value, jnp.zeros_like(value)
            )
    width = inv_ref.shape[0]
    picked = picked_ref[...]
    for i in range(width // tile):
        rows = pl.ds(i * tile, tile)
        update = lax.dot_general(
            factor_ref[:, i * tile : (i + 1) * tile],
            picked,
            (((0,), (0,)), ((), ())),
            preferred_element_type=jnp.float32,
        )
        reduced_ref[rows, :] = (rhs_ref[rows, :].astype(jnp.float32) - update).astype(jnp.bfloat16)
    solve_rows(inv_ref, reduced_ref, x_ref, piece_refs, chip, tile)


def select_kernel(old_count, index_ref, *refs):
    pools, outs = refs[:-CHIPS], refs[-CHIPS:]
    slots = outs[0].shape[0]
    for relative, out_ref in enumerate(outs):
        for slot in range(slots):
            place = index_ref[relative, slot]
            value, base = None, 0
            for pool in pools:
                size = pool.shape[0]
                local = place - base
                found = pool[jnp.clip(local, 0, size - 1)]
                value = found if value is None else jnp.where(local >= 0, found, value)
                base += size
            out_ref[slot] = value


def solve_columns(rhs, inv_diag, factor, places, infos):
    levels, width, columns = rhs.shape
    slots = places.shape[2]
    tile = factor.shape[1] // slots
    per_node = width // tile
    quarter = tile // CHIPS
    piece = jax.ShapeDtypeStruct((per_node, quarter, columns), jnp.bfloat16)
    solved = jax.ShapeDtypeStruct((width, columns), jnp.float32)
    part = jax.ShapeDtypeStruct((slots, quarter, columns), jnp.bfloat16)
    params = pltpu.CompilerParams(vmem_limit_bytes=32 * 2**20)
    old = []
    outputs = []
    solve_flops = 2 * width * width * columns
    for level in range(levels):
        last = level == levels - 1
        shapes = (solved,) if last else (solved,) + (piece,) * CHIPS
        if level == 0:
            results = pl.pallas_call(
                functools.partial(first_kernel, tile),
                out_shape=shapes,
                in_specs=[SMEM, VMEM, VMEM],
                out_specs=[VMEM] * len(shapes),
                compiler_params=params,
                cost_estimate=pl.CostEstimate(
                    flops=solve_flops, bytes_accessed=2 * width * (width + 4 * columns), transcendentals=0
                ),
                name="first",
            )(infos[0], rhs[0], inv_diag[0])
        else:
            pools = old + fresh
            parts = pl.pallas_call(
                functools.partial(select_kernel, 0),
                out_shape=(part,) * CHIPS,
                in_specs=[SMEM] + [VMEM] * len(pools),
                out_specs=[VMEM] * CHIPS,
                compiler_params=params,
                cost_estimate=pl.CostEstimate(
                    flops=0, bytes_accessed=4 * slots * tile * columns, transcendentals=0
                ),
                name=f"select{level}",
            )(places[level - 1], *pools)
            received = [parts[0]] + [send(parts[hop], hop) for hop in range(1, CHIPS)]
            results = pl.pallas_call(
                functools.partial(level_kernel, tile),
                out_shape=shapes,
                in_specs=[SMEM] + [VMEM] * (3 + CHIPS),
                out_specs=[VMEM] * len(shapes),
                scratch_shapes=[
                    pltpu.VMEM((slots * tile, columns), jnp.bfloat16),
                    pltpu.VMEM((width, columns), jnp.bfloat16),
                ],
                compiler_params=params,
                cost_estimate=pl.CostEstimate(
                    flops=solve_flops + 2 * slots * tile * width * columns,
                    bytes_accessed=2 * slots * tile * (width + columns),
                    transcendentals=0,
                ),
                name=f"level{level}",
            )(infos[level], rhs[level], factor[level - 1], inv_diag[level], *received)
            if not last:
                old = [jnp.concatenate(old + fresh, 0)]
        outputs.append(results[0])
        if not last:
            pieces = results[1:]
            own = [pieces[0]]
            for hop in range(1, CHIPS):
                own.append(send(pieces[hop], hop))
            previous = [send(pieces[hop], hop, 1) for hop in range(CHIPS)]
            own = jnp.concatenate(own, 0)
            previous = jnp.concatenate(previous, 0)
            fresh = [previous, swap(previous), own, swap(own)]
    return outputs


def body(rhs, inv_diag, factor, tile_list, live_count):
    width_k = rhs.shape[2]
    width = rhs.shape[1]
    slots = tile_list.shape[2]
    per_node = width // (factor.shape[1] // slots)
    position = lax.axis_index("nodes") % GROUP
    chip, core = position // CORES, position % CORES

    own_list = tile_list[:, 0]
    lists = jnp.stack([own_list] + [send(own_list, hop) for hop in range(1, CHIPS)], 1)
    pool = 2 * GROUP * per_node
    level, inside = lists // pool, lists % pool
    group, inside = inside // (GROUP * per_node), inside % (GROUP * per_node)
    member, row = inside // per_node, inside % per_node
    half = 2 * group + ((member % CORES) ^ core)
    places = level * pool + (half * CHIPS + ((member // CORES) ^ chip)) * per_node + row
    infos = [jnp.stack([chip, jnp.int32(0)])] + [
        jnp.stack([chip, live_count[i, 0]]) for i in range(live_count.shape[0])
    ]

    step = width_k // STREAMS
    streams = [
        solve_columns(rhs[:, :, s * step : (s + 1) * step], inv_diag, factor, places, infos)
        for s in range(STREAMS)
    ]
    return jnp.concatenate([jnp.stack(stream) for stream in streams], 2)


def solution(mesh):
    return jax.shard_map(
        body,
        mesh=mesh,
        in_specs=(
            P(None, "nodes", None),
            P(None, "nodes", None),
            P(None, "nodes", None),
            P(None, "nodes", None),
            P(None, "nodes"),
        ),
        out_specs=P(None, "nodes", None),
        check_vma=False,
    )
```

```python
import functools

import jax
import jax.numpy as jnp
from jax import lax
from jax.experimental import pallas as pl
from jax.experimental.pallas import tpu as pltpu
from jax.sharding import PartitionSpec as P

GROUP = 8
CORES = 2
CHIPS = GROUP // CORES


HBM = pl.BlockSpec(memory_space=pltpu.HBM)
VMEM = pl.BlockSpec(memory_space=pltpu.VMEM)
SMEM = pl.BlockSpec(memory_space=pltpu.SMEM)
PARAMS = pltpu.CompilerParams(vmem_limit_bytes=16 * 2**20)


def send(value, hop, step=0):
    size = lax.axis_size("nodes")
    route = [(i, ((i ^ (hop * CORES)) + step * GROUP) % size) for i in range(size)]
    return lax.ppermute(value, "nodes", route)


def swap(value):
    size = lax.axis_size("nodes")
    return lax.ppermute(value, "nodes", [(i, i ^ 1) for i in range(size)])


def cost(flops, moved):
    return pl.CostEstimate(flops=flops, bytes_accessed=moved, transcendentals=0)


def chip_place():
    return lax.axis_index("nodes") % GROUP // CORES


def solve_rows(inv_ref, reduced_ref, x_ref, piece_refs, tile, row_done=None):
    width = inv_ref.shape[0]
    quarter = tile // CHIPS
    per_node = width // tile
    for i in reversed(range(per_node)):
        x_ref[i * tile : (i + 1) * tile, :] = jnp.dot(
            inv_ref[i * tile : (i + 1) * tile, i * tile :],
            reduced_ref[i * tile :, :],
            preferred_element_type=jnp.float32,
        )
        if row_done is not None:
            row_done(i)
    for relative, piece_ref in enumerate(piece_refs):
        first = (chip_place() ^ relative) * quarter
        for i in range(per_node):
            start = pl.multiple_of(i * tile + first, quarter)
            piece_ref[i] = x_ref[pl.ds(start, quarter), :].astype(jnp.bfloat16)


def first_kernel(tile, rhs_hbm, inv_hbm, x_ref, *refs):
    piece_refs, (rhs_ref, inv_ref, sems) = refs[:-3], refs[-3:]
    copies = [
        pltpu.make_async_copy(rhs_hbm.at[0], rhs_ref, sems.at[0]),
        pltpu.make_async_copy(inv_hbm.at[0], inv_ref, sems.at[1]),
    ]
    for copy in copies:
        copy.start()
    for copy in copies:
        copy.wait()
    solve_rows(inv_ref, rhs_ref, x_ref, piece_refs, tile)


def load_kernel(level, after_ref, rhs_hbm, inv_hbm, factor_hbm, rhs_ref, inv_ref, factor_ref, sems):
    copies = [
        pltpu.make_async_copy(rhs_hbm.at[level], rhs_ref, sems.at[0]),
        pltpu.make_async_copy(inv_hbm.at[level], inv_ref, sems.at[1]),
        pltpu.make_async_copy(factor_hbm.at[level - 1], factor_ref, sems.at[2]),
    ]
    for copy in copies:
        copy.start()
    for copy in copies:
        copy.wait()


def store_kernel(level, x_ref, *refs):
    out_hbm, sem = refs[-2:]
    copy = pltpu.make_async_copy(x_ref, out_hbm.at[level], sem)
    copy.start()
    copy.wait()


def pack_kernel(*refs):
    out_ref = refs[-1]
    base = 0
    for ref in refs[:-1]:
        out_ref[base : base + ref.shape[0]] = ref[...]
        base += ref.shape[0]


def level_kernel(level, levels, tile, places_ref, rhs_ref, inv_ref, factor_ref, *refs):
    parts, refs = refs[:CHIPS], refs[CHIPS:]
    last = level == levels - 1
    picked_ref, reduced_ref = refs[-2:] if not last else refs[-4:-2]
    count = places_ref[places_ref.shape[0] - levels + level]
    slots, quarter = parts[0].shape[:2]
    for relative, part in enumerate(parts):
        first = (chip_place() ^ relative) * quarter
        for slot in range(slots):
            start = pl.multiple_of(slot * tile + first, quarter)
            value = part[slot]
            picked_ref[pl.ds(start, quarter), :] = jnp.where(
                slot < count, value, jnp.zeros_like(value)
            )
    width = inv_ref.shape[0]
    picked = picked_ref[...]
    for i in range(width // tile):
        rows = slice(i * tile, (i + 1) * tile)
        update = lax.dot_general(
            factor_ref[:, rows],
            picked,
            (((0,), (0,)), ((), ())),
            preferred_element_type=jnp.float32,
        )
        reduced_ref[rows, :] = (rhs_ref[rows, :].astype(jnp.float32) - update).astype(jnp.bfloat16)
    if not last:
        solve_rows(inv_ref, reduced_ref, refs[0], refs[1:-2], tile)
        return
    out_hbm, x_ref, sems = refs[1], refs[-2], refs[-1]

    def row_copy(i):
        rows = pl.ds(i * tile, tile)
        return pltpu.make_async_copy(x_ref.at[rows], out_hbm.at[level, rows], sems.at[i])

    solve_rows(inv_ref, reduced_ref, x_ref, (), tile, lambda i: row_copy(i).start())
    for i in range(width // tile):
        row_copy(i).wait()


def select_kernel(level, places_ref, *refs):
    pools, outs = refs[:-CHIPS], refs[-CHIPS:]
    slots = outs[0].shape[0]
    for relative, out_ref in enumerate(outs):
        for slot in range(slots):
            place = places_ref[(level - 1) * CHIPS * slots + relative * slots + slot]
            value, base = None, 0
            for pool in pools:
                size = pool.shape[0]
                local = place - base
                found = pool[jnp.clip(local, 0, size - 1)]
                value = found if value is None else jnp.where(local >= 0, found, value)
                base += size
            out_ref[slot] = value


def body(rhs, inv_diag, factor, tile_list, live_count):
    levels, width, columns = rhs.shape
    slots = tile_list.shape[2]
    tile = factor.shape[1] // slots
    per_node = width // tile
    quarter = tile // CHIPS
    half = jnp.bfloat16
    piece = jax.ShapeDtypeStruct((per_node, quarter, columns), half)
    solved = jax.ShapeDtypeStruct((width, columns), jnp.float32)
    part = jax.ShapeDtypeStruct((slots, quarter, columns), half)
    out_shape = jax.ShapeDtypeStruct((levels, width, columns), jnp.float32)
    solve_flops = width * width * columns
    level_flops = solve_flops + 2 * slots * tile * width * columns
    semaphores = pltpu.SemaphoreType.DMA

    rhs, inv_diag, factor = (
        pltpu.with_memory_space_constraint(value, pltpu.HBM) for value in (rhs, inv_diag, factor)
    )
    position = lax.axis_index("nodes") % GROUP
    chip, core = position // CORES, position % CORES
    own_list = tile_list[:, 0]
    lists = jnp.stack([own_list] + [send(own_list, hop) for hop in range(1, CHIPS)], 1)
    pool = 2 * GROUP * per_node
    named, inside = lists // pool, lists % pool
    group, inside = inside // (GROUP * per_node), inside % (GROUP * per_node)
    member, row = inside // per_node, inside % per_node
    side = 2 * group + ((member % CORES) ^ core)
    places = named * pool + (side * CHIPS + ((member // CORES) ^ chip)) * per_node + row
    places = jnp.concatenate([places.reshape(-1), live_count.reshape(-1)])

    old, fresh, out = [], [], None
    for level in range(levels):
        last = level == levels - 1
        if level == 0:
            shapes = (solved,) + (piece,) * CHIPS
            solution, *pieces = pl.pallas_call(
                functools.partial(first_kernel, tile),
                out_shape=shapes,
                in_specs=[HBM, HBM],
                out_specs=[VMEM] * len(shapes),
                scratch_shapes=[
                    pltpu.VMEM((width, columns), half),
                    pltpu.VMEM((width, width), half),
                    semaphores((2,)),
                ],
                compiler_params=PARAMS,
                cost_estimate=cost(solve_flops, 2 * width * (width + 4 * columns)),
                name="first",
            )(rhs, inv_diag)
        else:
            pools = old + fresh
            parts = pl.pallas_call(
                functools.partial(select_kernel, level),
                out_shape=(part,) * CHIPS,
                in_specs=[SMEM] + [VMEM] * len(pools),
                out_specs=[VMEM] * CHIPS,
                compiler_params=PARAMS,
                cost_estimate=cost(0, 4 * slots * tile * columns),
                name=f"select{level}",
            )(places, *pools)
            received = [parts[0]] + [send(parts[hop], hop) for hop in range(1, CHIPS)]
            if not last:
                old = old + [
                    pl.pallas_call(
                        pack_kernel,
                        out_shape=jax.ShapeDtypeStruct((pool, quarter, columns), half),
                        in_specs=[VMEM] * len(fresh),
                        out_specs=VMEM,
                        compiler_params=PARAMS,
                        cost_estimate=cost(0, 4 * pool * quarter * columns),
                        name=f"pack{level}",
                    )(*fresh)
                ]
            operands = (places,) + weights + tuple(received)
            scratch = [
                pltpu.VMEM((slots * tile, columns), half),
                pltpu.VMEM((width, columns), half),
            ]
            moved = 2 * slots * tile * (width + columns)
            call = functools.partial(
                pl.pallas_call,
                functools.partial(level_kernel, level, levels, tile),
                compiler_params=PARAMS,
                cost_estimate=cost(level_flops, moved),
                name=f"level{level}",
            )
            in_specs = [SMEM] + [VMEM] * (len(operands) - 1)
            if last:
                return call(
                    out_shape=out_shape,
                    in_specs=in_specs + [HBM],
                    out_specs=HBM,
                    input_output_aliases={len(operands): 0},
                    scratch_shapes=scratch
                    + [pltpu.VMEM((width, columns), jnp.float32), semaphores((per_node,))],
                )(*operands, out)
            shapes = (solved,) + (piece,) * CHIPS
            solution, *pieces = call(
                out_shape=shapes,
                in_specs=in_specs,
                out_specs=[VMEM] * len(shapes),
                scratch_shapes=scratch,
            )(*operands)
        previous = [send(pieces[hop], hop, 1) for hop in range(CHIPS)]
        own = [pieces[0]] + [send(pieces[hop], hop) for hop in range(1, CHIPS)]
        weights = tuple(
            pl.pallas_call(
                functools.partial(load_kernel, level + 1),
                out_shape=(
                    jax.ShapeDtypeStruct((width, columns), half),
                    jax.ShapeDtypeStruct((width, width), half),
                    jax.ShapeDtypeStruct((slots * tile, width), half),
                ),
                in_specs=[HBM] * 4,
                out_specs=[VMEM] * 3,
                scratch_shapes=[semaphores((3,))],
                compiler_params=PARAMS,
                cost_estimate=cost(0, 2 * width * (columns + width + slots * tile)),
                name=f"load{level + 1}",
            )(pieces[0], rhs, inv_diag, factor)
        )
        out = pl.pallas_call(
            functools.partial(store_kernel, level),
            out_shape=out_shape,
            in_specs=[VMEM] if level == 0 else [VMEM, HBM],
            out_specs=HBM,
            input_output_aliases={} if level == 0 else {1: 0},
            scratch_shapes=[semaphores],
            compiler_params=PARAMS,
            cost_estimate=cost(0, 4 * width * columns),
            name=f"store{level}",
        )(*((solution,) if level == 0 else (solution, out)))
        own = jnp.concatenate(own, 0)
        previous = jnp.concatenate(previous, 0)
        fresh = [previous, swap(previous), own, swap(own)]


def solution(mesh):
    return jax.shard_map(
        body,
        mesh=mesh,
        in_specs=(
            P(None, "nodes", None),
            P(None, "nodes", None),
            P(None, "nodes", None),
            P(None, "nodes", None),
            P(None, "nodes"),
        ),
        out_specs=P(None, "nodes", None),
        check_vma=False,
    )
```

```python
import functools

import jax
import jax.numpy as jnp
from jax import lax
from jax.experimental import pallas as pl
from jax.experimental.pallas import tpu as pltpu
from jax.sharding import PartitionSpec as P

GROUP = 8
CORES = 2
CHIPS = GROUP // CORES


HBM = pl.BlockSpec(memory_space=pltpu.HBM)
VMEM = pl.BlockSpec(memory_space=pltpu.VMEM)
SMEM = pl.BlockSpec(memory_space=pltpu.SMEM)
PARAMS = pltpu.CompilerParams(vmem_limit_bytes=16 * 2**20)


LATE = (2, 3)
ORDER = tuple(hop for hop in range(CHIPS) if hop not in LATE) + LATE


def send(value, hop, step=0):
    size = lax.axis_size("nodes")
    route = [(i, ((i ^ (hop * CORES)) + step * GROUP) % size) for i in range(size)]
    return lax.ppermute(value, "nodes", route)


def swap(value):
    size = lax.axis_size("nodes")
    return lax.ppermute(value, "nodes", [(i, i ^ 1) for i in range(size)])


def call(kernel, out_shape, in_specs, out_specs, flops, moved, scratch=(), aliases=None):
    return pl.pallas_call(
        kernel,
        out_shape=out_shape,
        in_specs=in_specs,
        out_specs=out_specs,
        scratch_shapes=list(scratch),
        input_output_aliases=aliases or {},
        compiler_params=PARAMS,
        cost_estimate=pl.CostEstimate(flops=flops, bytes_accessed=moved, transcendentals=0),
    )


def chip_place():
    return lax.axis_index("nodes") % GROUP // CORES


def run_copies(copies):
    for copy in copies:
        copy.start()
    for copy in copies:
        copy.wait()


def solve_rows(inv_ref, reduced_ref, x_ref, piece_refs, tile, row_done=None):
    width = inv_ref.shape[0]
    quarter = tile // CHIPS
    per_node = width // tile
    for i in reversed(range(per_node)):
        x_ref[i * tile : (i + 1) * tile, :] = jnp.dot(
            inv_ref[i * tile : (i + 1) * tile, i * tile :],
            reduced_ref[i * tile :, :],
            preferred_element_type=jnp.float32,
        )
        if row_done is not None:
            row_done(i)
    for relative, piece_ref in enumerate(piece_refs):
        first = (chip_place() ^ relative) * quarter
        for i in range(per_node):
            start = pl.multiple_of(i * tile + first, quarter)
            piece_ref[i] = x_ref[pl.ds(start, quarter), :].astype(jnp.bfloat16)


def first_kernel(tile, list_ref, rhs_hbm, inv_hbm, x_ref, *refs):
    piece_refs, noted_refs = refs[:CHIPS], refs[CHIPS:-4]
    rhs_ref, inv_ref, note_ref, sems = refs[-4:]
    copies = [
        pltpu.make_async_copy(rhs_hbm.at[0], rhs_ref, sems.at[0]),
        pltpu.make_async_copy(inv_hbm.at[0], inv_ref, sems.at[1]),
    ]
    for copy in copies:
        copy.start()
    levels, _, slots = list_ref.shape
    note_ref[...] = jnp.zeros_like(note_ref)
    for level in range(levels):
        note_ref[level : level + 1, :slots] = list_ref[level].astype(jnp.float32)
    note = note_ref[...].astype(jnp.bfloat16)
    for copy in copies:
        copy.wait()
    solve_rows(inv_ref, rhs_ref, x_ref, piece_refs, tile)
    for piece_ref, noted_ref in zip(piece_refs[1:], noted_refs):
        per_node = piece_ref.shape[0]
        noted_ref[:per_node] = piece_ref[...]
        noted_ref[per_node] = note


def load_kernel(level, after_ref, rhs_hbm, inv_hbm, factor_hbm, rhs_ref, inv_ref, turned_ref, *scratch):
    factor_ref, sems = scratch
    copies = [
        pltpu.make_async_copy(
            factor_hbm.at[level - 1, :, chip_place() ^ relative],
            factor_ref.at[place],
            sems.at[place],
        )
        for place, relative in enumerate(ORDER)
    ] + [
        pltpu.make_async_copy(rhs_hbm.at[level], rhs_ref, sems.at[CHIPS]),
        pltpu.make_async_copy(inv_hbm.at[level], inv_ref, sems.at[CHIPS + 1]),
    ]
    for copy in copies:
        copy.start()
    for relative in range(CHIPS):
        copies[relative].wait()
        slots, quarter, width = factor_ref.shape[1:]
        depth = slots * quarter
        turned_ref[:, relative * depth : (relative + 1) * depth] = (
            factor_ref[relative].reshape(depth, width).T
        )
    for copy in copies[CHIPS:]:
        copy.wait()


def store_kernel(level, x_ref, *refs):
    out_hbm, sem = refs[-2:]
    run_copies([pltpu.make_async_copy(x_ref, out_hbm.at[level], sem)])


def live_part(level, count_ref, part_ref):
    slots, quarter, columns = part_ref.shape
    count = count_ref[:, level - 1 : level]
    part = part_ref[...].reshape(slots * quarter, columns)
    slot_row = lax.broadcasted_iota(jnp.int32, part.shape, 0)
    return jnp.where(slot_row < count * quarter, part, jnp.zeros_like(part))


def less_update(level, relatives, count_ref, base_ref, turned_ref, part_refs, joined_ref, out_ref):
    depth = joined_ref.shape[0] // len(relatives)
    for index, part_ref in enumerate(part_refs):
        joined_ref[index * depth : (index + 1) * depth, :] = live_part(
            level, count_ref, part_ref
        )
    first = ORDER.index(relatives[0]) * depth
    update = jnp.dot(
        turned_ref[:, first : first + joined_ref.shape[0]],
        joined_ref[...],
        preferred_element_type=jnp.float32,
    )
    out_ref[...] = (base_ref[...].astype(jnp.float32) - update).astype(out_ref.dtype)


def update_kernel(level, relatives, count_ref, base_ref, turned_ref, *refs):
    parts, (out_ref, joined_ref) = refs[:-2], refs[-2:]
    less_update(
        level, relatives, count_ref, base_ref, turned_ref, parts, joined_ref, out_ref
    )


def level_kernel(level, levels, tile, relatives, count_ref, base_ref, inv_ref, turned_ref, *refs):
    last = level == levels - 1
    parts, refs = refs[: len(relatives)], refs[len(relatives) :]
    joined_ref, reduced_ref = refs[-2:]
    refs = refs[:-1]
    less_update(
        level, relatives, count_ref, base_ref, turned_ref, parts, joined_ref, reduced_ref
    )
    if not last:
        solve_rows(inv_ref, reduced_ref, refs[0], refs[1:-1], tile)
        return
    out_hbm, x_ref, sems = refs[1:-1]

    def row_copy(i):
        rows = pl.ds(i * tile, tile)
        return pltpu.make_async_copy(x_ref.at[rows], out_hbm.at[level, rows], sems.at[i])

    solve_rows(inv_ref, reduced_ref, x_ref, (), tile, lambda i: row_copy(i).start())
    for i in range(inv_ref.shape[0] // tile):
        row_copy(i).wait()


def select_kernel(level, last, places_ref, *refs):
    old, fresh = refs[: level - 1], refs[level - 1 : -CHIPS - 1]
    pool_ref, outs = (refs[-1], refs[-CHIPS - 1 : -1]) if last else (refs[-CHIPS - 1], refs[-CHIPS:])
    step = pool_ref.shape[0] // len(fresh)
    for place, ref in enumerate(fresh):
        pool_ref[place * step : (place + 1) * step] = ref[:step]
    size = pool_ref.shape[0]
    slots = outs[0].shape[0]
    named = places_ref[level - 1 : level, :]
    for relative, out_ref in enumerate(outs):
        for slot in range(slots):
            place = named[0, relative * slots + slot]
            if level == 1:
                out_ref[slot] = pool_ref[place]
                continue
            value = None
            for index, pool in enumerate(old + (pool_ref,)):
                local = place - index * size
                found = pool[jnp.clip(local, 0, size - 1)]
                value = found if value is None else jnp.where(local >= 0, found, value)
            out_ref[slot] = value


def body(rhs, inv_diag, factor, tile_list, live_count):
    levels, width, columns = rhs.shape
    slots = tile_list.shape[2]
    tile = factor.shape[1] // slots
    per_node = width // tile
    quarter = tile // CHIPS
    pool = 2 * GROUP * per_node
    half = jnp.bfloat16
    piece = jax.ShapeDtypeStruct((per_node, quarter, columns), half)
    solved = jax.ShapeDtypeStruct((width, columns), jnp.float32)
    part = jax.ShapeDtypeStruct((slots, quarter, columns), half)
    out_shape = jax.ShapeDtypeStruct((levels, width, columns), jnp.float32)
    solve_flops = width * width * columns
    part_flops = 2 * slots * quarter * width * columns
    part_moved = 2 * slots * quarter * (width + columns) + 8 * width * columns
    semaphores = pltpu.SemaphoreType.DMA

    rhs, inv_diag, factor = (
        pltpu.with_memory_space_constraint(value, pltpu.HBM)
        for value in (rhs, inv_diag, factor.reshape(-1, slots, CHIPS, quarter, width))
    )

    assert (levels - 1) * pool <= 256 and levels - 1 <= quarter and slots <= columns
    shapes = (solved,) + (piece,) * CHIPS
    noted = jax.ShapeDtypeStruct((per_node + 1, quarter, columns), half)
    solution, *outputs = call(
        functools.partial(first_kernel, tile),
        shapes + (noted,) * (CHIPS - 1),
        [VMEM, HBM, HBM],
        [VMEM] * (len(shapes) + CHIPS - 1),
        solve_flops,
        2 * width * (width + 4 * columns),
        [
            pltpu.VMEM((width, columns), half),
            pltpu.VMEM((width, width), half),
            pltpu.VMEM((quarter, columns), jnp.float32),
            semaphores((2,)),
        ],
    )(tile_list, rhs, inv_diag)
    pieces, noted = outputs[:CHIPS], outputs[CHIPS:]

    position = lax.axis_index("nodes") % GROUP
    chip, core = position // CORES, position % CORES
    own = [pieces[0]] + [send(value, hop) for hop, value in zip(range(1, CHIPS), noted)]
    notes = [value[per_node, : levels - 1, :slots] for value in [noted[0]] + own[1:]]
    lists = jnp.stack(notes, 1).astype(jnp.int32)
    named, inside = lists // pool, lists % pool
    group, inside = inside // (GROUP * per_node), inside % (GROUP * per_node)
    member, row = inside // per_node, inside % per_node
    side = 2 * group + ((member % CORES) ^ core)
    places = named * pool + (side * CHIPS + ((member // CORES) ^ chip)) * per_node + row
    places = places.reshape(levels - 1, CHIPS * slots)
    counts = live_count.T

    pools = []
    for level in range(1, levels):
        last = level == levels - 1
        previous = [send(pieces[hop], hop, 1) for hop in range(CHIPS)]
        if level > 1:
            own = [pieces[0]] + [send(pieces[hop], hop) for hop in range(1, CHIPS)]
        rhs_here, inv_here, turned = call(
            functools.partial(load_kernel, level),
            (
                jax.ShapeDtypeStruct((width, columns), half),
                jax.ShapeDtypeStruct((width, width), half),
                jax.ShapeDtypeStruct((width, slots * tile), half),
            ),
            [HBM] * 4,
            [VMEM] * 3,
            0,
            2 * width * (columns + width + slots * tile),
            [pltpu.VMEM((CHIPS, slots, quarter, width), half), semaphores((2 + CHIPS,))],
        )(pieces[0], rhs, inv_diag, factor)
        out = call(
            functools.partial(store_kernel, level - 1),
            out_shape,
            [VMEM] if level == 1 else [VMEM, HBM],
            HBM,
            0,
            4 * width * columns,
            [semaphores],
            {} if level == 1 else {1: 0},
        )(*((solution,) if level == 1 else (solution, out)))
        fresh = previous + [swap(value) for value in previous] + own + [swap(value) for value in own]

        inputs = pools + fresh
        packed = jax.ShapeDtypeStruct((pool, quarter, columns), half)
        selected = call(
            functools.partial(select_kernel, level, last),
            (part,) * CHIPS if last else (packed,) + (part,) * CHIPS,
            [VMEM] * (1 + len(inputs)),
            [VMEM] * (CHIPS if last else 1 + CHIPS),
            0,
            4 * (slots * CHIPS + pool) * quarter * columns,
            [pltpu.VMEM(packed.shape, half)] if last else [],
        )(places, *inputs)
        pools, parts = pools + list(selected[:-CHIPS]), selected[-CHIPS:]
        parts = [parts[0]] + [send(parts[hop], hop) for hop in range(1, CHIPS)]
        late = LATE
        early = tuple(hop for hop in range(CHIPS) if hop not in late)
        base = call(
            functools.partial(update_kernel, level, early),
            solved,
            [VMEM] * (3 + len(early)),
            VMEM,
            part_flops * len(early),
            part_moved * len(early),
            [pltpu.VMEM((len(early) * slots * quarter, columns), half)],
        )(counts, rhs_here, turned, *[parts[hop] for hop in early])
        level_call = functools.partial(
            call,
            functools.partial(level_kernel, level, levels, tile, late),
            flops=solve_flops + part_flops * len(late),
            moved=part_moved * len(late),
        )
        operands = (counts, base, inv_here, turned) + tuple(parts[hop] for hop in late)
        in_specs = [VMEM] * len(operands)
        joined = pltpu.VMEM((len(late) * slots * quarter, columns), half)
        reduced = pltpu.VMEM((width, columns), half)
        if last:
            return level_call(
                out_shape=out_shape,
                in_specs=in_specs + [HBM],
                out_specs=HBM,
                scratch=[pltpu.VMEM((width, columns), jnp.float32), semaphores((per_node,)), joined, reduced],
                aliases={len(operands): 0},
            )(*operands, out)
        solution, *pieces = level_call(
            out_shape=shapes,
            in_specs=in_specs,
            out_specs=[VMEM] * len(shapes),
            scratch=[joined, reduced],
        )(*operands)


def solution(mesh):
    return jax.shard_map(
        body,
        mesh=mesh,
        in_specs=(
            P(None, "nodes", None),
            P(None, "nodes", None),
            P(None, "nodes", None),
            P(None, "nodes", None),
            P(None, "nodes"),
        ),
        out_specs=P(None, "nodes", None),
        check_vma=False,
    )
```

```python
import functools

import jax
import jax.numpy as jnp
from jax import lax
from jax.experimental import pallas as pl
from jax.experimental.pallas import tpu as pltpu
from jax.sharding import PartitionSpec as P

GROUP = 8
CORES = 2
CHIPS = GROUP // CORES


HBM = pl.BlockSpec(memory_space=pltpu.HBM)
VMEM = pl.BlockSpec(memory_space=pltpu.VMEM)
SMEM = pl.BlockSpec(memory_space=pltpu.SMEM)
PARAMS = pltpu.CompilerParams(vmem_limit_bytes=16 * 2**20)


LATE = (2, 3)
ORDER = tuple(hop for hop in range(CHIPS) if hop not in LATE) + LATE


def send(value, hop, step=0):
    size = lax.axis_size("nodes")
    route = [(i, ((i ^ (hop * CORES)) + step * GROUP) % size) for i in range(size)]
    return lax.ppermute(value, "nodes", route)


def swap(value):
    size = lax.axis_size("nodes")
    return lax.ppermute(value, "nodes", [(i, i ^ 1) for i in range(size)])


def call(kernel, out_shape, in_specs, out_specs, flops, moved, scratch=(), aliases=None):
    return pl.pallas_call(
        kernel,
        out_shape=out_shape,
        in_specs=in_specs,
        out_specs=out_specs,
        scratch_shapes=list(scratch),
        input_output_aliases=aliases or {},
        compiler_params=PARAMS,
        cost_estimate=pl.CostEstimate(flops=flops, bytes_accessed=moved, transcendentals=0),
    )


def chip_place():
    return lax.axis_index("nodes") % GROUP // CORES


def run_copies(copies):
    for copy in copies:
        copy.start()
    for copy in copies:
        copy.wait()


def solve_rows(inv_ref, reduced_ref, x_ref, piece_refs, tile, row_done=None):
    width = inv_ref.shape[0]
    quarter = tile // CHIPS
    per_node = width // tile
    for i in reversed(range(per_node)):
        x_ref[i * tile : (i + 1) * tile, :] = jnp.dot(
            inv_ref[i * tile : (i + 1) * tile, i * tile :],
            reduced_ref[i * tile :, :],
            preferred_element_type=jnp.float32,
        )
        if row_done is not None:
            row_done(i)
    for relative, piece_ref in enumerate(piece_refs):
        first = (chip_place() ^ relative) * quarter
        for i in range(per_node):
            start = pl.multiple_of(i * tile + first, quarter)
            piece_ref[i] = x_ref[pl.ds(start, quarter), :].astype(jnp.bfloat16)


def first_kernel(tile, list_hbm, rhs_hbm, inv_hbm, x_ref, *refs):
    piece_refs, noted_refs = refs[:CHIPS], refs[CHIPS:-5]
    rhs_ref, inv_ref, list_ref, note_ref, sems = refs[-5:]
    copies = [
        pltpu.make_async_copy(rhs_hbm.at[0], rhs_ref, sems.at[0]),
        pltpu.make_async_copy(inv_hbm.at[0], inv_ref, sems.at[1]),
        pltpu.make_async_copy(list_hbm, list_ref, sems.at[2]),
    ]
    for copy in copies:
        copy.start()
    for copy in copies:
        copy.wait()
    levels, _, slots = list_ref.shape
    note_ref[...] = jnp.zeros_like(note_ref)
    for level in range(levels):
        note_ref[level : level + 1, :slots] = list_ref[level].astype(jnp.float32)
    note = note_ref[...].astype(jnp.bfloat16)
    solve_rows(inv_ref, rhs_ref, x_ref, piece_refs, tile)
    for piece_ref, noted_ref in zip(piece_refs[1:], noted_refs):
        per_node = piece_ref.shape[0]
        noted_ref[:per_node] = piece_ref[...]
        noted_ref[per_node] = note


def load_kernel(level, after_ref, rhs_hbm, inv_hbm, factor_hbm, rhs_ref, inv_ref, turned_ref, *scratch):
    factor_ref, sems = scratch
    copies = [
        pltpu.make_async_copy(
            factor_hbm.at[level - 1, :, chip_place() ^ relative],
            factor_ref.at[place],
            sems.at[place],
        )
        for place, relative in enumerate(ORDER)
    ] + [
        pltpu.make_async_copy(rhs_hbm.at[level], rhs_ref, sems.at[CHIPS]),
        pltpu.make_async_copy(inv_hbm.at[level], inv_ref, sems.at[CHIPS + 1]),
    ]
    for copy in copies:
        copy.start()
    for relative in range(CHIPS):
        copies[relative].wait()
        slots, quarter, width = factor_ref.shape[1:]
        depth = slots * quarter
        turned_ref[:, relative * depth : (relative + 1) * depth] = (
            factor_ref[relative].reshape(depth, width).T
        )
    for copy in copies[CHIPS:]:
        copy.wait()


def store_kernel(level, x_ref, *refs):
    out_hbm, sem = refs[-2:]
    run_copies([pltpu.make_async_copy(x_ref, out_hbm.at[level], sem)])


def live_part(level, count_ref, part_ref):
    slots, quarter, columns = part_ref.shape
    count = count_ref[:, level - 1 : level]
    part = part_ref[...].reshape(slots * quarter, columns)
    slot_row = lax.broadcasted_iota(jnp.int32, part.shape, 0)
    return jnp.where(slot_row < count * quarter, part, jnp.zeros_like(part))


def less_update(level, relatives, count_ref, base_ref, turned_ref, part_refs, joined_ref, out_ref):
    depth = joined_ref.shape[0] // len(relatives)
    for index, part_ref in enumerate(part_refs):
        joined_ref[index * depth : (index + 1) * depth, :] = live_part(
            level, count_ref, part_ref
        )
    first = ORDER.index(relatives[0]) * depth
    update = jnp.dot(
        turned_ref[:, first : first + joined_ref.shape[0]],
        joined_ref[...],
        preferred_element_type=jnp.float32,
    )
    out_ref[...] = (base_ref[...].astype(jnp.float32) - update).astype(out_ref.dtype)


def update_kernel(level, relatives, count_ref, base_ref, turned_ref, *refs):
    parts, (out_ref, joined_ref) = refs[:-2], refs[-2:]
    less_update(
        level, relatives, count_ref, base_ref, turned_ref, parts, joined_ref, out_ref
    )


def level_kernel(level, levels, tile, relatives, count_ref, base_ref, inv_ref, turned_ref, *refs):
    last = level == levels - 1
    parts, refs = refs[: len(relatives)], refs[len(relatives) :]
    joined_ref, reduced_ref = refs[-2:]
    refs = refs[:-1]
    less_update(
        level, relatives, count_ref, base_ref, turned_ref, parts, joined_ref, reduced_ref
    )
    if not last:
        solve_rows(inv_ref, reduced_ref, refs[0], refs[1:-1], tile)
        return
    out_hbm, x_ref, sems = refs[1:-1]

    def row_copy(i):
        rows = pl.ds(i * tile, tile)
        return pltpu.make_async_copy(x_ref.at[rows], out_hbm.at[level, rows], sems.at[i])

    solve_rows(inv_ref, reduced_ref, x_ref, (), tile, lambda i: row_copy(i).start())
    for i in range(inv_ref.shape[0] // tile):
        row_copy(i).wait()


def select_kernel(level, last, places_ref, *refs):
    old, fresh = refs[: level - 1], refs[level - 1 : -CHIPS - 1]
    pool_ref, outs = (refs[-1], refs[-CHIPS - 1 : -1]) if last else (refs[-CHIPS - 1], refs[-CHIPS:])
    step = pool_ref.shape[0] // len(fresh)
    for place, ref in enumerate(fresh):
        pool_ref[place * step : (place + 1) * step] = ref[:step]
    size = pool_ref.shape[0]
    slots = outs[0].shape[0]
    named = places_ref[level - 1 : level, :]
    for relative, out_ref in enumerate(outs):
        for slot in range(slots):
            place = named[0, relative * slots + slot]
            if level == 1:
                out_ref[slot] = pool_ref[place]
                continue
            value = None
            for index, pool in enumerate(old + (pool_ref,)):
                local = place - index * size
                found = pool[jnp.clip(local, 0, size - 1)]
                value = found if value is None else jnp.where(local >= 0, found, value)
            out_ref[slot] = value


def body(rhs, inv_diag, factor, tile_list, live_count):
    levels, width, columns = rhs.shape
    slots = tile_list.shape[2]
    tile = factor.shape[1] // slots
    per_node = width // tile
    quarter = tile // CHIPS
    pool = 2 * GROUP * per_node
    half = jnp.bfloat16
    piece = jax.ShapeDtypeStruct((per_node, quarter, columns), half)
    solved = jax.ShapeDtypeStruct((width, columns), jnp.float32)
    part = jax.ShapeDtypeStruct((slots, quarter, columns), half)
    out_shape = jax.ShapeDtypeStruct((levels, width, columns), jnp.float32)
    solve_flops = width * width * columns
    part_flops = 2 * slots * quarter * width * columns
    part_moved = 2 * slots * quarter * (width + columns) + 8 * width * columns
    semaphores = pltpu.SemaphoreType.DMA

    rhs, inv_diag, factor, tile_list = (
        pltpu.with_memory_space_constraint(value, pltpu.HBM)
        for value in (
            rhs,
            inv_diag,
            factor.reshape(-1, slots, CHIPS, quarter, width),
            tile_list,
        )
    )

    assert (levels - 1) * pool <= 256 and levels - 1 <= quarter and slots <= columns
    shapes = (solved,) + (piece,) * CHIPS
    noted = jax.ShapeDtypeStruct((per_node + 1, quarter, columns), half)
    solution, *outputs = call(
        functools.partial(first_kernel, tile),
        shapes + (noted,) * (CHIPS - 1),
        [HBM] * 3,
        [VMEM] * (len(shapes) + CHIPS - 1),
        solve_flops,
        2 * width * (width + 4 * columns),
        [
            pltpu.VMEM((width, columns), half),
            pltpu.VMEM((width, width), half),
            pltpu.VMEM(tile_list.shape, jnp.int32),
            pltpu.VMEM((quarter, columns), jnp.float32),
            semaphores((3,)),
        ],
    )(tile_list, rhs, inv_diag)
    pieces, noted = outputs[:CHIPS], outputs[CHIPS:]

    position = lax.axis_index("nodes") % GROUP
    chip, core = position // CORES, position % CORES
    own = [pieces[0]] + [send(value, hop) for hop, value in zip(range(1, CHIPS), noted)]
    notes = [value[per_node, : levels - 1, :slots] for value in [noted[0]] + own[1:]]
    lists = jnp.stack(notes, 1).astype(jnp.int32)
    named, inside = lists // pool, lists % pool
    group, inside = inside // (GROUP * per_node), inside % (GROUP * per_node)
    member, row = inside // per_node, inside % per_node
    side = 2 * group + ((member % CORES) ^ core)
    places = named * pool + (side * CHIPS + ((member // CORES) ^ chip)) * per_node + row
    places = places.reshape(levels - 1, CHIPS * slots)
    counts = live_count.T

    pools = []
    for level in range(1, levels):
        last = level == levels - 1
        previous = [send(pieces[hop], hop, 1) for hop in range(CHIPS)]
        if level > 1:
            own = [pieces[0]] + [send(pieces[hop], hop) for hop in range(1, CHIPS)]
        rhs_here, inv_here, turned = call(
            functools.partial(load_kernel, level),
            (
                jax.ShapeDtypeStruct((width, columns), half),
                jax.ShapeDtypeStruct((width, width), half),
                jax.ShapeDtypeStruct((width, slots * tile), half),
            ),
            [HBM] * 4,
            [VMEM] * 3,
            0,
            2 * width * (columns + width + slots * tile),
            [pltpu.VMEM((CHIPS, slots, quarter, width), half), semaphores((2 + CHIPS,))],
        )(pieces[0], rhs, inv_diag, factor)
        out = call(
            functools.partial(store_kernel, level - 1),
            out_shape,
            [VMEM] if level == 1 else [VMEM, HBM],
            HBM,
            0,
            4 * width * columns,
            [semaphores],
            {} if level == 1 else {1: 0},
        )(*((solution,) if level == 1 else (solution, out)))
        fresh = (
            previous
            + [swap(value) for value in previous]
            + own
            + [swap(value) for value in own]
        )

        inputs = pools + fresh
        packed = jax.ShapeDtypeStruct((pool, quarter, columns), half)
        selected = call(
            functools.partial(select_kernel, level, last),
            (part,) * CHIPS if last else (packed,) + (part,) * CHIPS,
            [VMEM] * (1 + len(inputs)),
            [VMEM] * (CHIPS if last else 1 + CHIPS),
            0,
            4 * (slots * CHIPS + pool) * quarter * columns,
            [pltpu.VMEM(packed.shape, half)] if last else [],
        )(places, *inputs)
        pools, parts = pools + list(selected[:-CHIPS]), selected[-CHIPS:]
        parts = [parts[0]] + [send(parts[hop], hop) for hop in range(1, CHIPS)]
        late = LATE
        early = tuple(hop for hop in range(CHIPS) if hop not in late)
        base = call(
            functools.partial(update_kernel, level, early),
            solved,
            [VMEM] * (3 + len(early)),
            VMEM,
            part_flops * len(early),
            part_moved * len(early),
            [pltpu.VMEM((len(early) * slots * quarter, columns), half)],
        )(counts, rhs_here, turned, *[parts[hop] for hop in early])
        level_call = functools.partial(
            call,
            functools.partial(level_kernel, level, levels, tile, late),
            flops=solve_flops + part_flops * len(late),
            moved=part_moved * len(late),
        )
        operands = (counts, base, inv_here, turned) + tuple(parts[hop] for hop in late)
        in_specs = [VMEM] * len(operands)
        joined = pltpu.VMEM((len(late) * slots * quarter, columns), half)
        reduced = pltpu.VMEM((width, columns), half)
        if last:
            return level_call(
                out_shape=out_shape,
                in_specs=in_specs + [HBM],
                out_specs=HBM,
                scratch=[pltpu.VMEM((width, columns), jnp.float32), semaphores((per_node,)), joined, reduced],
                aliases={len(operands): 0},
            )(*operands, out)
        solution, *pieces = level_call(
            out_shape=shapes,
            in_specs=in_specs,
            out_specs=[VMEM] * len(shapes),
            scratch=[joined, reduced],
        )(*operands)


def solution(mesh):
    return jax.shard_map(
        body,
        mesh=mesh,
        in_specs=(
            P(None, "nodes", None),
            P(None, "nodes", None),
            P(None, "nodes", None),
            P(None, "nodes", None),
            P(None, "nodes"),
        ),
        out_specs=P(None, "nodes", None),
        check_vma=False,
    )
```

```python
import functools

import jax
import jax.numpy as jnp
from jax import lax
from jax.experimental import pallas as pl
from jax.experimental.pallas import tpu as pltpu
from jax.sharding import PartitionSpec as P

GROUP = 8
CORES = 2
CHIPS = GROUP // CORES


HBM = pl.BlockSpec(memory_space=pltpu.HBM)
VMEM = pl.BlockSpec(memory_space=pltpu.VMEM)
SMEM = pl.BlockSpec(memory_space=pltpu.SMEM)
PARAMS = pltpu.CompilerParams(vmem_limit_bytes=16 * 2**20)


LATE = (2, 3)
ORDER = tuple(hop for hop in range(CHIPS) if hop not in LATE) + LATE


def send(value, hop, step=0):
    size = lax.axis_size("nodes")
    route = [(i, ((i ^ (hop * CORES)) + step * GROUP) % size) for i in range(size)]
    return lax.ppermute(value, "nodes", route)


def swap(value):
    size = lax.axis_size("nodes")
    return lax.ppermute(value, "nodes", [(i, i ^ 1) for i in range(size)])


def call(kernel, out_shape, in_specs, out_specs, flops, moved, scratch=(), aliases=None):
    return pl.pallas_call(
        kernel,
        out_shape=out_shape,
        in_specs=in_specs,
        out_specs=out_specs,
        scratch_shapes=list(scratch),
        input_output_aliases=aliases or {},
        compiler_params=PARAMS,
        cost_estimate=pl.CostEstimate(flops=flops, bytes_accessed=moved, transcendentals=0),
    )


def chip_place():
    return lax.axis_index("nodes") % GROUP // CORES


def run_copies(copies):
    for copy in copies:
        copy.start()
    for copy in copies:
        copy.wait()


def solve_rows(inv_ref, reduced_ref, x_ref, piece_refs, tile, row_done=None):
    width = inv_ref.shape[0]
    quarter = tile // CHIPS
    per_node = width // tile
    for i in reversed(range(per_node)):
        x_ref[i * tile : (i + 1) * tile, :] = jnp.dot(
            inv_ref[i * tile : (i + 1) * tile, i * tile :],
            reduced_ref[i * tile :, :],
            preferred_element_type=jnp.float32,
        )
        if row_done is not None:
            row_done(i)
    for relative, piece_ref in enumerate(piece_refs):
        first = (chip_place() ^ relative) * quarter
        for i in range(per_node):
            start = pl.multiple_of(i * tile + first, quarter)
            piece_ref[i] = x_ref[pl.ds(start, quarter), :].astype(jnp.bfloat16)


def places_of(entries, relative, levels, pool, per_node):
    def whole_parts(value, size, most):
        return sum((value >= size * k).astype(jnp.int32) for k in range(1, most))

    position = lax.axis_index("nodes") % GROUP
    chip, core = position // CORES, position % CORES
    named = whole_parts(entries, pool, levels)
    inside = entries - named * pool
    group = whole_parts(inside, GROUP * per_node, 2)
    inside = inside - group * (GROUP * per_node)
    member = whole_parts(inside, per_node, GROUP)
    row = inside - member * per_node
    member_chip = whole_parts(member, CORES, CHIPS)
    side = CORES * group + ((member - member_chip * CORES) ^ core)
    return named * pool + (side * CHIPS + (member_chip ^ (chip ^ relative))) * per_node + row


def first_kernel(tile, list_hbm, rhs_hbm, inv_hbm, x_ref, *refs):
    piece_refs, noted_refs = refs[:CHIPS], refs[CHIPS:-5]
    rhs_ref, inv_ref, list_ref, note_ref, sems = refs[-5:]
    run_copies(
        [
            pltpu.make_async_copy(rhs_hbm.at[0], rhs_ref, sems.at[0]),
            pltpu.make_async_copy(inv_hbm.at[0], inv_ref, sems.at[1]),
            pltpu.make_async_copy(list_hbm, list_ref, sems.at[2]),
        ]
    )
    levels, _, slots = list_ref.shape
    per_node = inv_ref.shape[0] // tile
    pool = 2 * GROUP * per_node
    solve_rows(inv_ref, rhs_ref, x_ref, piece_refs, tile)
    note_ref[...] = jnp.zeros_like(note_ref)
    for relative in range(CHIPS):
        for level in range(levels):
            places = places_of(list_ref[level], relative, levels, pool, per_node)
            note_ref[level : level + 1, :slots] = places.astype(jnp.float32)
        noted_refs[relative][:per_node] = piece_refs[relative][...]
        noted_refs[relative][per_node] = note_ref[...].astype(jnp.bfloat16)


def load_kernel(level, after_ref, rhs_hbm, inv_hbm, factor_hbm, rhs_ref, inv_ref, turned_ref, *scratch):
    factor_ref, sems = scratch
    copies = [
        pltpu.make_async_copy(
            factor_hbm.at[level - 1, :, chip_place() ^ relative],
            factor_ref.at[place],
            sems.at[place],
        )
        for place, relative in enumerate(ORDER)
    ] + [
        pltpu.make_async_copy(rhs_hbm.at[level], rhs_ref, sems.at[CHIPS]),
        pltpu.make_async_copy(inv_hbm.at[level], inv_ref, sems.at[CHIPS + 1]),
    ]
    for copy in copies:
        copy.start()
    for relative in range(CHIPS):
        copies[relative].wait()
        slots, quarter, width = factor_ref.shape[1:]
        depth = slots * quarter
        turned_ref[:, relative * depth : (relative + 1) * depth] = (
            factor_ref[relative].reshape(depth, width).T
        )
    for copy in copies[CHIPS:]:
        copy.wait()


def store_kernel(level, x_ref, *refs):
    out_hbm, sem = refs[-2:]
    run_copies([pltpu.make_async_copy(x_ref, out_hbm.at[level], sem)])


def live_part(level, count_ref, part_ref):
    slots, quarter, columns = part_ref.shape
    count = count_ref[:, level - 1 : level]
    part = part_ref[...].reshape(slots * quarter, columns)
    slot_row = lax.broadcasted_iota(jnp.int32, part.shape, 0)
    return jnp.where(slot_row < count * quarter, part, jnp.zeros_like(part))


def less_update(level, relatives, count_ref, base_ref, turned_ref, part_refs, joined_ref, out_ref):
    depth = joined_ref.shape[0] // len(relatives)
    for index, part_ref in enumerate(part_refs):
        joined_ref[index * depth : (index + 1) * depth, :] = live_part(
            level, count_ref, part_ref
        )
    first = ORDER.index(relatives[0]) * depth
    update = jnp.dot(
        turned_ref[:, first : first + joined_ref.shape[0]],
        joined_ref[...],
        preferred_element_type=jnp.float32,
    )
    out_ref[...] = (base_ref[...].astype(jnp.float32) - update).astype(out_ref.dtype)


def update_kernel(level, relatives, count_ref, base_ref, turned_ref, *refs):
    parts, (out_ref, joined_ref) = refs[:-2], refs[-2:]
    less_update(
        level, relatives, count_ref, base_ref, turned_ref, parts, joined_ref, out_ref
    )


def level_kernel(level, levels, tile, relatives, count_ref, base_ref, inv_ref, turned_ref, *refs):
    last = level == levels - 1
    parts, refs = refs[: len(relatives)], refs[len(relatives) :]
    joined_ref, reduced_ref = refs[-2:]
    refs = refs[:-1]
    less_update(
        level, relatives, count_ref, base_ref, turned_ref, parts, joined_ref, reduced_ref
    )
    if not last:
        solve_rows(inv_ref, reduced_ref, refs[0], refs[1:-1], tile)
        return
    out_hbm, x_ref, sems = refs[1:-1]

    def row_copy(i):
        rows = pl.ds(i * tile, tile)
        return pltpu.make_async_copy(x_ref.at[rows], out_hbm.at[level, rows], sems.at[i])

    solve_rows(inv_ref, reduced_ref, x_ref, (), tile, lambda i: row_copy(i).start())
    for i in range(inv_ref.shape[0] // tile):
        row_copy(i).wait()


def select_kernel(level, last, *refs):
    notes, refs = refs[:CHIPS], refs[CHIPS:]
    old, fresh = refs[: level - 1], refs[level - 1 : -CHIPS - 1]
    pool_ref, outs = (refs[-1], refs[-CHIPS - 1 : -1]) if last else (refs[-CHIPS - 1], refs[-CHIPS:])
    step = pool_ref.shape[0] // len(fresh)
    for place, ref in enumerate(fresh):
        pool_ref[place * step : (place + 1) * step] = ref[:step]
    size = pool_ref.shape[0]
    slots = outs[0].shape[0]
    for relative, out_ref in enumerate(outs):
        note = notes[relative][notes[relative].shape[0] - 1].astype(jnp.float32)
        places = note[:, :128].astype(jnp.int32)
        for slot in range(slots):
            place = places[level - 1, slot]
            if level == 1:
                out_ref[slot] = pool_ref[place]
                continue
            value = None
            for index, pool in enumerate(old + (pool_ref,)):
                local = place - index * size
                found = pool[jnp.clip(local, 0, size - 1)]
                value = found if value is None else jnp.where(local >= 0, found, value)
            out_ref[slot] = value


def body(rhs, inv_diag, factor, tile_list, live_count):
    levels, width, columns = rhs.shape
    slots = tile_list.shape[2]
    tile = factor.shape[1] // slots
    per_node = width // tile
    quarter = tile // CHIPS
    pool = 2 * GROUP * per_node
    half = jnp.bfloat16
    piece = jax.ShapeDtypeStruct((per_node, quarter, columns), half)
    solved = jax.ShapeDtypeStruct((width, columns), jnp.float32)
    part = jax.ShapeDtypeStruct((slots, quarter, columns), half)
    out_shape = jax.ShapeDtypeStruct((levels, width, columns), jnp.float32)
    solve_flops = width * width * columns
    part_flops = 2 * slots * quarter * width * columns
    part_moved = 2 * slots * quarter * (width + columns) + 8 * width * columns
    semaphores = pltpu.SemaphoreType.DMA

    rhs, inv_diag, factor, tile_list = (
        pltpu.with_memory_space_constraint(value, pltpu.HBM)
        for value in (
            rhs,
            inv_diag,
            factor.reshape(-1, slots, CHIPS, quarter, width),
            tile_list,
        )
    )

    assert (levels - 1) * pool <= 256 and levels - 1 <= quarter and slots <= columns
    shapes = (solved,) + (piece,) * CHIPS
    noted = jax.ShapeDtypeStruct((per_node + 1, quarter, columns), half)
    solution, *outputs = call(
        functools.partial(first_kernel, tile),
        shapes + (noted,) * CHIPS,
        [HBM] * 3,
        [VMEM] * (len(shapes) + CHIPS),
        solve_flops,
        2 * width * (width + 4 * columns),
        [
            pltpu.VMEM((width, columns), half),
            pltpu.VMEM((width, width), half),
            pltpu.VMEM(tile_list.shape, jnp.int32),
            pltpu.VMEM((quarter, columns), jnp.float32),
            semaphores((3,)),
        ],
    )(tile_list, rhs, inv_diag)
    pieces, noted = outputs[:CHIPS], outputs[CHIPS:]

    own = [noted[0]] + [send(noted[hop], hop) for hop in range(1, CHIPS)]
    notes = own
    counts = live_count.T

    pools = []
    for level in range(1, levels):
        last = level == levels - 1
        previous = [send(pieces[hop], hop, 1) for hop in range(CHIPS)]
        if level > 1:
            own = [pieces[0]] + [send(pieces[hop], hop) for hop in range(1, CHIPS)]
        rhs_here, inv_here, turned = call(
            functools.partial(load_kernel, level),
            (
                jax.ShapeDtypeStruct((width, columns), half),
                jax.ShapeDtypeStruct((width, width), half),
                jax.ShapeDtypeStruct((width, slots * tile), half),
            ),
            [HBM] * 4,
            [VMEM] * 3,
            0,
            2 * width * (columns + width + slots * tile),
            [pltpu.VMEM((CHIPS, slots, quarter, width), half), semaphores((2 + CHIPS,))],
        )(pieces[0], rhs, inv_diag, factor)
        out = call(
            functools.partial(store_kernel, level - 1),
            out_shape,
            [VMEM] if level == 1 else [VMEM, HBM],
            HBM,
            0,
            4 * width * columns,
            [semaphores],
            {} if level == 1 else {1: 0},
        )(*((solution,) if level == 1 else (solution, out)))
        fresh = (
            previous
            + [swap(value) for value in previous]
            + own
            + [swap(value) for value in own]
        )

        inputs = pools + fresh
        packed = jax.ShapeDtypeStruct((pool, quarter, columns), half)
        selected = call(
            functools.partial(select_kernel, level, last),
            (part,) * CHIPS if last else (packed,) + (part,) * CHIPS,
            [VMEM] * (CHIPS + len(inputs)),
            [VMEM] * (CHIPS if last else 1 + CHIPS),
            0,
            4 * (slots * CHIPS + pool) * quarter * columns,
            [pltpu.VMEM(packed.shape, half)] if last else [],
        )(*notes, *inputs)
        pools, parts = pools + list(selected[:-CHIPS]), selected[-CHIPS:]
        parts = [parts[0]] + [send(parts[hop], hop) for hop in range(1, CHIPS)]
        late = LATE
        early = tuple(hop for hop in range(CHIPS) if hop not in late)
        base = call(
            functools.partial(update_kernel, level, early),
            solved,
            [VMEM] * (3 + len(early)),
            VMEM,
            part_flops * len(early),
            part_moved * len(early),
            [pltpu.VMEM((len(early) * slots * quarter, columns), half)],
        )(counts, rhs_here, turned, *[parts[hop] for hop in early])
        level_call = functools.partial(
            call,
            functools.partial(level_kernel, level, levels, tile, late),
            flops=solve_flops + part_flops * len(late),
            moved=part_moved * len(late),
        )
        operands = (counts, base, inv_here, turned) + tuple(parts[hop] for hop in late)
        in_specs = [VMEM] * len(operands)
        joined = pltpu.VMEM((len(late) * slots * quarter, columns), half)
        reduced = pltpu.VMEM((width, columns), half)
        if last:
            return level_call(
                out_shape=out_shape,
                in_specs=in_specs + [HBM],
                out_specs=HBM,
                scratch=[pltpu.VMEM((width, columns), jnp.float32), semaphores((per_node,)), joined, reduced],
                aliases={len(operands): 0},
            )(*operands, out)
        solution, *pieces = level_call(
            out_shape=shapes,
            in_specs=in_specs,
            out_specs=[VMEM] * len(shapes),
            scratch=[joined, reduced],
        )(*operands)


def solution(mesh):
    return jax.shard_map(
        body,
        mesh=mesh,
        in_specs=(
            P(None, "nodes", None),
            P(None, "nodes", None),
            P(None, "nodes", None),
            P(None, "nodes", None),
            P(None, "nodes"),
        ),
        out_specs=P(None, "nodes", None),
        check_vma=False,
    )
```

```python
import functools

import jax
import jax.numpy as jnp
from jax import lax
from jax.experimental import pallas as pl
from jax.experimental.pallas import tpu as pltpu
from jax.sharding import PartitionSpec as P

GROUP = 8
CORES = 2
CHIPS = GROUP // CORES


HBM = pl.BlockSpec(memory_space=pltpu.HBM)
VMEM = pl.BlockSpec(memory_space=pltpu.VMEM)
SMEM = pl.BlockSpec(memory_space=pltpu.SMEM)
PARAMS = pltpu.CompilerParams(vmem_limit_bytes=16 * 2**20)


LATE = (2, 3)
ORDER = tuple(hop for hop in range(CHIPS) if hop not in LATE) + LATE


def send(value, hop, step=0):
    size = lax.axis_size("nodes")
    route = [(i, ((i ^ (hop * CORES)) + step * GROUP) % size) for i in range(size)]
    return lax.ppermute(value, "nodes", route)


def swap(value):
    size = lax.axis_size("nodes")
    return lax.ppermute(value, "nodes", [(i, i ^ 1) for i in range(size)])


def call(kernel, out_shape, in_specs, out_specs, flops, moved, scratch=(), aliases=None):
    return pl.pallas_call(
        kernel,
        out_shape=out_shape,
        in_specs=in_specs,
        out_specs=out_specs,
        scratch_shapes=list(scratch),
        input_output_aliases=aliases or {},
        compiler_params=PARAMS,
        cost_estimate=pl.CostEstimate(flops=flops, bytes_accessed=moved, transcendentals=0),
    )


def chip_place():
    return lax.axis_index("nodes") % GROUP // CORES


def run_copies(copies):
    for copy in copies:
        copy.start()
    for copy in copies:
        copy.wait()


def solve_rows(inv_ref, reduced_ref, x_ref, piece_refs, tile, row_done=None):
    width = inv_ref.shape[0]
    quarter = tile // CHIPS
    per_node = width // tile
    for i in reversed(range(per_node)):
        x_ref[i * tile : (i + 1) * tile, :] = jnp.dot(
            inv_ref[i * tile : (i + 1) * tile, i * tile :],
            reduced_ref[i * tile :, :],
            preferred_element_type=jnp.float32,
        )
        if row_done is not None:
            row_done(i)
    for relative, piece_ref in enumerate(piece_refs):
        first = (chip_place() ^ relative) * quarter
        for i in range(per_node):
            start = pl.multiple_of(i * tile + first, quarter)
            piece_ref[i] = x_ref[pl.ds(start, quarter), :].astype(jnp.bfloat16)


def places_of(entries, relative, levels, pool, per_node):
    def whole_parts(value, size, most):
        return sum((value >= size * k).astype(jnp.int32) for k in range(1, most))

    position = lax.axis_index("nodes") % GROUP
    chip, core = position // CORES, position % CORES
    named = whole_parts(entries, pool, levels)
    inside = entries - named * pool
    group = whole_parts(inside, GROUP * per_node, 2)
    inside = inside - group * (GROUP * per_node)
    member = whole_parts(inside, per_node, GROUP)
    row = inside - member * per_node
    member_chip = whole_parts(member, CORES, CHIPS)
    side = CORES * group + ((member - member_chip * CORES) ^ core)
    return named * pool + (side * CHIPS + (member_chip ^ (chip ^ relative))) * per_node + row


def first_kernel(tile, list_hbm, rhs_hbm, inv_hbm, x_ref, *refs):
    piece_refs, noted_refs = refs[:CHIPS], refs[CHIPS:-5]
    rhs_ref, inv_ref, list_ref, note_ref, sems = refs[-5:]
    run_copies(
        [
            pltpu.make_async_copy(rhs_hbm.at[0], rhs_ref, sems.at[0]),
            pltpu.make_async_copy(inv_hbm.at[0], inv_ref, sems.at[1]),
            pltpu.make_async_copy(list_hbm, list_ref, sems.at[2]),
        ]
    )
    levels, _, slots = list_ref.shape
    per_node = inv_ref.shape[0] // tile
    pool = 2 * GROUP * per_node
    solve_rows(inv_ref, rhs_ref, x_ref, piece_refs, tile)
    note_ref[...] = jnp.zeros_like(note_ref)
    for relative in range(CHIPS):
        for level in range(levels):
            places = places_of(list_ref[level], relative, levels, pool, per_node)
            note_ref[level : level + 1, :slots] = places.astype(jnp.float32)
        noted_refs[relative][:per_node] = piece_refs[relative][...]
        noted_refs[relative][per_node] = note_ref[...].astype(jnp.bfloat16)


def load_kernel(level, after_ref, rhs_hbm, inv_hbm, factor_hbm, rhs_ref, inv_ref, turned_ref, *scratch):
    factor_ref, sems = scratch
    copies = [
        pltpu.make_async_copy(
            factor_hbm.at[level - 1, :, chip_place() ^ relative],
            factor_ref.at[place],
            sems.at[place],
        )
        for place, relative in enumerate(ORDER)
    ] + [
        pltpu.make_async_copy(rhs_hbm.at[level], rhs_ref, sems.at[CHIPS]),
        pltpu.make_async_copy(inv_hbm.at[level], inv_ref, sems.at[CHIPS + 1]),
    ]
    for copy in copies:
        copy.start()
    for relative in range(CHIPS):
        copies[relative].wait()
        slots, quarter, width = factor_ref.shape[1:]
        depth = slots * quarter
        turned_ref[:, relative * depth : (relative + 1) * depth] = (
            factor_ref[relative].reshape(depth, width).T
        )
    for copy in copies[CHIPS:]:
        copy.wait()


def store_kernel(level, x_ref, *refs):
    out_hbm, sem = refs[-2:]
    run_copies([pltpu.make_async_copy(x_ref, out_hbm.at[level], sem)])


def live_part(level, count_ref, part_ref):
    slots, quarter, columns = part_ref.shape
    count = count_ref[:, level - 1 : level]
    part = part_ref[...].reshape(slots * quarter, columns)
    slot_row = lax.broadcasted_iota(jnp.int32, part.shape, 0)
    return jnp.where(slot_row < count * quarter, part, jnp.zeros_like(part))


def less_update(level, relatives, count_ref, base_ref, turned_ref, part_refs, joined_ref, out_ref):
    depth = joined_ref.shape[0] // len(relatives)
    for index, part_ref in enumerate(part_refs):
        joined_ref[index * depth : (index + 1) * depth, :] = live_part(
            level, count_ref, part_ref
        )
    first = ORDER.index(relatives[0]) * depth
    update = jnp.dot(
        turned_ref[:, first : first + joined_ref.shape[0]],
        joined_ref[...],
        preferred_element_type=jnp.float32,
    )
    out_ref[...] = (base_ref[...].astype(jnp.float32) - update).astype(out_ref.dtype)


def update_kernel(level, relatives, count_ref, base_ref, turned_ref, *refs):
    parts, (out_ref, joined_ref) = refs[:-2], refs[-2:]
    less_update(
        level, relatives, count_ref, base_ref, turned_ref, parts, joined_ref, out_ref
    )


def level_kernel(level, levels, tile, relatives, count_ref, base_ref, inv_ref, turned_ref, *refs):
    last = level == levels - 1
    parts, refs = refs[: len(relatives)], refs[len(relatives) :]
    joined_ref, reduced_ref = refs[-2:]
    refs = refs[:-1]
    less_update(
        level, relatives, count_ref, base_ref, turned_ref, parts, joined_ref, reduced_ref
    )
    if not last:
        solve_rows(inv_ref, reduced_ref, refs[0], refs[1:-1], tile)
        return
    out_hbm, x_ref, sems = refs[1:-1]

    def row_copy(i):
        rows = pl.ds(i * tile, tile)
        return pltpu.make_async_copy(x_ref.at[rows], out_hbm.at[level, rows], sems.at[i])

    solve_rows(inv_ref, reduced_ref, x_ref, (), tile, lambda i: row_copy(i).start())
    for i in range(inv_ref.shape[0] // tile):
        row_copy(i).wait()


def select_kernel(level, pool, *refs):
    notes, refs = refs[:CHIPS], refs[CHIPS + (level > 1) :]
    fresh, pool_ref, outs = refs[: -CHIPS - 1], refs[-CHIPS - 1], refs[-CHIPS:]
    step = pool // len(fresh)
    for place, ref in enumerate(fresh):
        first = (level - 1) * pool + place * step
        pool_ref[first : first + step] = ref[:step]
    slots = outs[0].shape[0]
    for relative, out_ref in enumerate(outs):
        note = notes[relative][notes[relative].shape[0] - 1].astype(jnp.float32)
        places = note[:, :128].astype(jnp.int32)
        for slot in range(slots):
            out_ref[slot] = pool_ref[places[level - 1, slot]]


def body(rhs, inv_diag, factor, tile_list, live_count):
    levels, width, columns = rhs.shape
    slots = tile_list.shape[2]
    tile = factor.shape[1] // slots
    per_node = width // tile
    quarter = tile // CHIPS
    pool = 2 * GROUP * per_node
    half = jnp.bfloat16
    piece = jax.ShapeDtypeStruct((per_node, quarter, columns), half)
    solved = jax.ShapeDtypeStruct((width, columns), jnp.float32)
    part = jax.ShapeDtypeStruct((slots, quarter, columns), half)
    out_shape = jax.ShapeDtypeStruct((levels, width, columns), jnp.float32)
    solve_flops = width * width * columns
    part_flops = 2 * slots * quarter * width * columns
    part_moved = 2 * slots * quarter * (width + columns) + 8 * width * columns
    semaphores = pltpu.SemaphoreType.DMA

    rhs, inv_diag, factor, tile_list = (
        pltpu.with_memory_space_constraint(value, pltpu.HBM)
        for value in (
            rhs,
            inv_diag,
            factor.reshape(-1, slots, CHIPS, quarter, width),
            tile_list,
        )
    )

    assert (levels - 1) * pool <= 256 and levels - 1 <= quarter and slots <= columns
    shapes = (solved,) + (piece,) * CHIPS
    noted = jax.ShapeDtypeStruct((per_node + 1, quarter, columns), half)
    solution, *outputs = call(
        functools.partial(first_kernel, tile),
        shapes + (noted,) * CHIPS,
        [HBM] * 3,
        [VMEM] * (len(shapes) + CHIPS),
        solve_flops,
        2 * width * (width + 4 * columns),
        [
            pltpu.VMEM((width, columns), half),
            pltpu.VMEM((width, width), half),
            pltpu.VMEM(tile_list.shape, jnp.int32),
            pltpu.VMEM((quarter, columns), jnp.float32),
            semaphores((3,)),
        ],
    )(tile_list, rhs, inv_diag)
    pieces, noted = outputs[:CHIPS], outputs[CHIPS:]

    own = [noted[0]] + [send(noted[hop], hop) for hop in range(1, CHIPS)]
    notes = own
    counts = live_count.T

    pools = []
    for level in range(1, levels):
        last = level == levels - 1
        previous = [send(pieces[hop], hop, 1) for hop in range(CHIPS)]
        if level > 1:
            own = [pieces[0]] + [send(pieces[hop], hop) for hop in range(1, CHIPS)]
        rhs_here, inv_here, turned = call(
            functools.partial(load_kernel, level),
            (
                jax.ShapeDtypeStruct((width, columns), half),
                jax.ShapeDtypeStruct((width, width), half),
                jax.ShapeDtypeStruct((width, slots * tile), half),
            ),
            [HBM] * 4,
            [VMEM] * 3,
            0,
            2 * width * (columns + width + slots * tile),
            [pltpu.VMEM((CHIPS, slots, quarter, width), half), semaphores((2 + CHIPS,))],
        )(pieces[0], rhs, inv_diag, factor)
        out = call(
            functools.partial(store_kernel, level - 1),
            out_shape,
            [VMEM] if level == 1 else [VMEM, HBM],
            HBM,
            0,
            4 * width * columns,
            [semaphores],
            {} if level == 1 else {1: 0},
        )(*((solution,) if level == 1 else (solution, out)))
        fresh = (
            previous
            + [swap(value) for value in previous]
            + own
            + [swap(value) for value in own]
        )

        inputs = pools + fresh
        packed = jax.ShapeDtypeStruct(((levels - 1) * pool, quarter, columns), half)
        packed, *parts = call(
            functools.partial(select_kernel, level, pool),
            (packed,) + (part,) * CHIPS,
            [VMEM] * (CHIPS + len(inputs)),
            [VMEM] * (1 + CHIPS),
            0,
            4 * (slots * CHIPS + pool) * quarter * columns,
            aliases={CHIPS: 0} if pools else {},
        )(*notes, *inputs)
        pools = [packed]
        parts = [parts[0]] + [send(parts[hop], hop) for hop in range(1, CHIPS)]
        late = LATE
        early = tuple(hop for hop in range(CHIPS) if hop not in late)
        base = call(
            functools.partial(update_kernel, level, early),
            solved,
            [VMEM] * (3 + len(early)),
            VMEM,
            part_flops * len(early),
            part_moved * len(early),
            [pltpu.VMEM((len(early) * slots * quarter, columns), half)],
        )(counts, rhs_here, turned, *[parts[hop] for hop in early])
        level_call = functools.partial(
            call,
            functools.partial(level_kernel, level, levels, tile, late),
            flops=solve_flops + part_flops * len(late),
            moved=part_moved * len(late),
        )
        operands = (counts, base, inv_here, turned) + tuple(parts[hop] for hop in late)
        in_specs = [VMEM] * len(operands)
        joined = pltpu.VMEM((len(late) * slots * quarter, columns), half)
        reduced = pltpu.VMEM((width, columns), half)
        if last:
            return level_call(
                out_shape=out_shape,
                in_specs=in_specs + [HBM],
                out_specs=HBM,
                scratch=[pltpu.VMEM((width, columns), jnp.float32), semaphores((per_node,)), joined, reduced],
                aliases={len(operands): 0},
            )(*operands, out)
        solution, *pieces = level_call(
            out_shape=shapes,
            in_specs=in_specs,
            out_specs=[VMEM] * len(shapes),
            scratch=[joined, reduced],
        )(*operands)


def solution(mesh):
    return jax.shard_map(
        body,
        mesh=mesh,
        in_specs=(
            P(None, "nodes", None),
            P(None, "nodes", None),
            P(None, "nodes", None),
            P(None, "nodes", None),
            P(None, "nodes"),
        ),
        out_specs=P(None, "nodes", None),
        check_vma=False,
    )
```

```python
import functools

import jax
import jax.numpy as jnp
from jax import lax
from jax.experimental import pallas as pl
from jax.experimental.pallas import tpu as pltpu
from jax.sharding import PartitionSpec as P

GROUP = 8
CORES = 2
CHIPS = GROUP // CORES


HBM = pl.BlockSpec(memory_space=pltpu.HBM)
VMEM = pl.BlockSpec(memory_space=pltpu.VMEM)
SMEM = pl.BlockSpec(memory_space=pltpu.SMEM)
PARAMS = pltpu.CompilerParams(vmem_limit_bytes=16 * 2**20)


LATE = (2, 3)
ORDER = tuple(hop for hop in range(CHIPS) if hop not in LATE) + LATE


def send(value, hop, step=0):
    size = lax.axis_size("nodes")
    route = [(i, ((i ^ (hop * CORES)) + step * GROUP) % size) for i in range(size)]
    return lax.ppermute(value, "nodes", route)


def swap(value):
    size = lax.axis_size("nodes")
    return lax.ppermute(value, "nodes", [(i, i ^ 1) for i in range(size)])


def call(kernel, out_shape, in_specs, out_specs, flops, moved, scratch=(), aliases=None):
    return pl.pallas_call(
        kernel,
        out_shape=out_shape,
        in_specs=in_specs,
        out_specs=out_specs,
        scratch_shapes=list(scratch),
        input_output_aliases=aliases or {},
        compiler_params=PARAMS,
        cost_estimate=pl.CostEstimate(flops=flops, bytes_accessed=moved, transcendentals=0),
    )


def chip_place():
    return lax.axis_index("nodes") % GROUP // CORES


def run_copies(copies):
    for copy in copies:
        copy.start()
    for copy in copies:
        copy.wait()


def solve_rows(inv_ref, reduced_ref, x_ref, piece_refs, tile, row_start=None, row_done=None):
    width = inv_ref.shape[0]
    quarter = tile // CHIPS
    per_node = width // tile
    for i in reversed(range(per_node)):
        if row_start is not None:
            row_start(i)
        x_ref[i * tile : (i + 1) * tile, :] = jnp.dot(
            inv_ref[i * tile : (i + 1) * tile, i * tile :],
            reduced_ref[i * tile :, :],
            preferred_element_type=jnp.float32,
        )
        if row_done is not None:
            row_done(i)
    for relative, piece_ref in enumerate(piece_refs):
        first = (chip_place() ^ relative) * quarter
        for i in range(per_node):
            start = pl.multiple_of(i * tile + first, quarter)
            piece_ref[i] = x_ref[pl.ds(start, quarter), :].astype(jnp.bfloat16)


def places_of(entries, relative, levels, pool, per_node):
    def whole_parts(value, size, most):
        return sum((value >= size * k).astype(jnp.int32) for k in range(1, most))

    position = lax.axis_index("nodes") % GROUP
    chip, core = position // CORES, position % CORES
    named = whole_parts(entries, pool, levels)
    inside = entries - named * pool
    group = whole_parts(inside, GROUP * per_node, 2)
    inside = inside - group * (GROUP * per_node)
    member = whole_parts(inside, per_node, GROUP)
    row = inside - member * per_node
    member_chip = whole_parts(member, CORES, CHIPS)
    side = CORES * group + ((member - member_chip * CORES) ^ core)
    return named * pool + (side * CHIPS + (member_chip ^ (chip ^ relative))) * per_node + row


def first_kernel(tile, list_hbm, rhs_hbm, inv_hbm, x_ref, *refs):
    piece_refs, noted_refs = refs[:CHIPS], refs[CHIPS:-5]
    rhs_ref, inv_ref, list_ref, note_ref, sems = refs[-5:]
    levels, _, slots = list_ref.shape
    width = inv_ref.shape[0]
    per_node = width // tile
    pool = 2 * GROUP * per_node
    split = (per_node + 1) // 2 * tile
    halves = [
        pltpu.make_async_copy(inv_hbm.at[0, pl.ds(first, size)], inv_ref.at[pl.ds(first, size)], sem)
        for first, size, sem in (
            (split, width - split, sems.at[0]),
            (0, split, sems.at[1]),
        )
    ]
    list_copy = pltpu.make_async_copy(list_hbm, list_ref, sems.at[2])
    rhs_copy = pltpu.make_async_copy(rhs_hbm.at[0], rhs_ref, sems.at[3])
    for copy in (list_copy, rhs_copy, *halves):
        copy.start()
    list_copy.wait()
    note_ref[...] = jnp.zeros_like(note_ref)
    for relative in range(CHIPS):
        for level in range(levels):
            places = places_of(list_ref[level], relative, levels, pool, per_node)
            note_ref[level : level + 1, :slots] = places.astype(jnp.float32)
        noted_refs[relative][per_node] = note_ref[...].astype(jnp.bfloat16)
    rhs_copy.wait()
    halves[0].wait()

    def row_start(i):
        if i == split // tile - 1:
            halves[1].wait()

    solve_rows(inv_ref, rhs_ref, x_ref, piece_refs, tile, row_start=row_start)
    for relative in range(CHIPS):
        noted_refs[relative][:per_node] = piece_refs[relative][...]


def load_kernel(level, after_ref, rhs_hbm, inv_hbm, factor_hbm, rhs_ref, inv_ref, turned_ref, *scratch):
    factor_ref, sems = scratch
    copies = [
        pltpu.make_async_copy(
            factor_hbm.at[level - 1, :, chip_place() ^ relative],
            factor_ref.at[place],
            sems.at[place],
        )
        for place, relative in enumerate(ORDER)
    ] + [
        pltpu.make_async_copy(rhs_hbm.at[level], rhs_ref, sems.at[CHIPS]),
        pltpu.make_async_copy(inv_hbm.at[level], inv_ref, sems.at[CHIPS + 1]),
    ]
    for copy in copies:
        copy.start()
    for relative in range(CHIPS):
        copies[relative].wait()
        slots, quarter, width = factor_ref.shape[1:]
        depth = slots * quarter
        turned_ref[:, relative * depth : (relative + 1) * depth] = (
            factor_ref[relative].reshape(depth, width).T
        )
    for copy in copies[CHIPS:]:
        copy.wait()


def store_kernel(level, x_ref, *refs):
    out_hbm, sem = refs[-2:]
    run_copies([pltpu.make_async_copy(x_ref, out_hbm.at[level], sem)])


def live_part(level, count_ref, part_ref):
    slots, quarter, columns = part_ref.shape
    count = count_ref[:, level - 1 : level]
    part = part_ref[...].reshape(slots * quarter, columns)
    slot_row = lax.broadcasted_iota(jnp.int32, part.shape, 0)
    return jnp.where(slot_row < count * quarter, part, jnp.zeros_like(part))


def less_update(level, relatives, count_ref, base_ref, turned_ref, part_refs, joined_ref, out_ref):
    depth = joined_ref.shape[0] // len(relatives)
    for index, part_ref in enumerate(part_refs):
        joined_ref[index * depth : (index + 1) * depth, :] = live_part(
            level, count_ref, part_ref
        )
    first = ORDER.index(relatives[0]) * depth
    update = jnp.dot(
        turned_ref[:, first : first + joined_ref.shape[0]],
        joined_ref[...],
        preferred_element_type=jnp.float32,
    )
    out_ref[...] = (base_ref[...].astype(jnp.float32) - update).astype(out_ref.dtype)


def update_kernel(level, relatives, count_ref, base_ref, turned_ref, *refs):
    parts, (out_ref, joined_ref) = refs[:-2], refs[-2:]
    less_update(
        level, relatives, count_ref, base_ref, turned_ref, parts, joined_ref, out_ref
    )


def level_kernel(level, levels, tile, relatives, count_ref, base_ref, inv_ref, turned_ref, *refs):
    last = level == levels - 1
    parts, refs = refs[: len(relatives)], refs[len(relatives) :]
    joined_ref, reduced_ref = refs[-2:]
    refs = refs[:-1]
    less_update(
        level, relatives, count_ref, base_ref, turned_ref, parts, joined_ref, reduced_ref
    )
    if not last:
        solve_rows(inv_ref, reduced_ref, refs[0], refs[1:-1], tile)
        return
    out_hbm, x_ref, sems = refs[1:-1]

    def row_copy(i):
        rows = pl.ds(i * tile, tile)
        return pltpu.make_async_copy(x_ref.at[rows], out_hbm.at[level, rows], sems.at[i])

    solve_rows(inv_ref, reduced_ref, x_ref, (), tile, row_done=lambda i: row_copy(i).start())
    for i in range(inv_ref.shape[0] // tile):
        row_copy(i).wait()


def select_kernel(level, pool, *refs):
    notes, refs = refs[:CHIPS], refs[CHIPS + (level > 1) :]
    fresh, pool_ref, outs = refs[: -CHIPS - 1], refs[-CHIPS - 1], refs[-CHIPS:]
    step = pool // len(fresh)
    for place, ref in enumerate(fresh):
        first = (level - 1) * pool + place * step
        pool_ref[first : first + step] = ref[:step]
    slots = outs[0].shape[0]
    for relative, out_ref in enumerate(outs):
        note = notes[relative][notes[relative].shape[0] - 1].astype(jnp.float32)
        places = note[:, :128].astype(jnp.int32)
        for slot in range(slots):
            out_ref[slot] = pool_ref[places[level - 1, slot]]


def body(rhs, inv_diag, factor, tile_list, live_count):
    levels, width, columns = rhs.shape
    slots = tile_list.shape[2]
    tile = factor.shape[1] // slots
    per_node = width // tile
    quarter = tile // CHIPS
    pool = 2 * GROUP * per_node
    half = jnp.bfloat16
    piece = jax.ShapeDtypeStruct((per_node, quarter, columns), half)
    solved = jax.ShapeDtypeStruct((width, columns), jnp.float32)
    part = jax.ShapeDtypeStruct((slots, quarter, columns), half)
    out_shape = jax.ShapeDtypeStruct((levels, width, columns), jnp.float32)
    solve_flops = width * width * columns
    part_flops = 2 * slots * quarter * width * columns
    part_moved = 2 * slots * quarter * (width + columns) + 8 * width * columns
    semaphores = pltpu.SemaphoreType.DMA

    rhs, inv_diag, factor, tile_list = (
        pltpu.with_memory_space_constraint(value, pltpu.HBM)
        for value in (
            rhs,
            inv_diag,
            factor.reshape(-1, slots, CHIPS, quarter, width),
            tile_list,
        )
    )

    assert (levels - 1) * pool <= 256 and levels - 1 <= quarter and slots <= columns
    shapes = (solved,) + (piece,) * CHIPS
    noted = jax.ShapeDtypeStruct((per_node + 1, quarter, columns), half)
    solution, *outputs = call(
        functools.partial(first_kernel, tile),
        shapes + (noted,) * CHIPS,
        [HBM] * 3,
        [VMEM] * (len(shapes) + CHIPS),
        solve_flops,
        2 * width * (width + 4 * columns),
        [
            pltpu.VMEM((width, columns), half),
            pltpu.VMEM((width, width), half),
            pltpu.VMEM(tile_list.shape, jnp.int32),
            pltpu.VMEM((quarter, columns), jnp.float32),
            semaphores((4,)),
        ],
    )(tile_list, rhs, inv_diag)
    pieces, noted = outputs[:CHIPS], outputs[CHIPS:]

    own = [noted[0]] + [send(noted[hop], hop) for hop in range(1, CHIPS)]
    notes = own
    counts = live_count.T

    pools = []
    for level in range(1, levels):
        last = level == levels - 1
        previous = [send(pieces[hop], hop, 1) for hop in range(CHIPS)]
        if level > 1:
            own = [pieces[0]] + [send(pieces[hop], hop) for hop in range(1, CHIPS)]
        rhs_here, inv_here, turned = call(
            functools.partial(load_kernel, level),
            (
                jax.ShapeDtypeStruct((width, columns), half),
                jax.ShapeDtypeStruct((width, width), half),
                jax.ShapeDtypeStruct((width, slots * tile), half),
            ),
            [HBM] * 4,
            [VMEM] * 3,
            0,
            2 * width * (columns + width + slots * tile),
            [pltpu.VMEM((CHIPS, slots, quarter, width), half), semaphores((2 + CHIPS,))],
        )(pieces[0], rhs, inv_diag, factor)
        out = call(
            functools.partial(store_kernel, level - 1),
            out_shape,
            [VMEM] if level == 1 else [VMEM, HBM],
            HBM,
            0,
            4 * width * columns,
            [semaphores],
            {} if level == 1 else {1: 0},
        )(*((solution,) if level == 1 else (solution, out)))
        fresh = (
            previous
            + [swap(value) for value in previous]
            + own
            + [swap(value) for value in own]
        )

        inputs = pools + fresh
        packed = jax.ShapeDtypeStruct(((levels - 1) * pool, quarter, columns), half)
        packed, *parts = call(
            functools.partial(select_kernel, level, pool),
            (packed,) + (part,) * CHIPS,
            [VMEM] * (CHIPS + len(inputs)),
            [VMEM] * (1 + CHIPS),
            0,
            4 * (slots * CHIPS + pool) * quarter * columns,
            aliases={CHIPS: 0} if pools else {},
        )(*notes, *inputs)
        pools = [packed]
        parts = [parts[0]] + [send(parts[hop], hop) for hop in range(1, CHIPS)]
        late = LATE
        early = tuple(hop for hop in range(CHIPS) if hop not in late)
        base = call(
            functools.partial(update_kernel, level, early),
            solved,
            [VMEM] * (3 + len(early)),
            VMEM,
            part_flops * len(early),
            part_moved * len(early),
            [pltpu.VMEM((len(early) * slots * quarter, columns), half)],
        )(counts, rhs_here, turned, *[parts[hop] for hop in early])
        level_call = functools.partial(
            call,
            functools.partial(level_kernel, level, levels, tile, late),
            flops=solve_flops + part_flops * len(late),
            moved=part_moved * len(late),
        )
        operands = (counts, base, inv_here, turned) + tuple(parts[hop] for hop in late)
        in_specs = [VMEM] * len(operands)
        joined = pltpu.VMEM((len(late) * slots * quarter, columns), half)
        reduced = pltpu.VMEM((width, columns), half)
        if last:
            return level_call(
                out_shape=out_shape,
                in_specs=in_specs + [HBM],
                out_specs=HBM,
                scratch=[pltpu.VMEM((width, columns), jnp.float32), semaphores((per_node,)), joined, reduced],
                aliases={len(operands): 0},
            )(*operands, out)
        solution, *pieces = level_call(
            out_shape=shapes,
            in_specs=in_specs,
            out_specs=[VMEM] * len(shapes),
            scratch=[joined, reduced],
        )(*operands)


def solution(mesh):
    return jax.shard_map(
        body,
        mesh=mesh,
        in_specs=(
            P(None, "nodes", None),
            P(None, "nodes", None),
            P(None, "nodes", None),
            P(None, "nodes", None),
            P(None, "nodes"),
        ),
        out_specs=P(None, "nodes", None),
        check_vma=False,
    )
```
